32 devices in a mesh: row: 8 (over z, x), col: 4 (over y, core).
Axes of the slice: x: 2, y: 2, z: 4, core: 2. Of those that a mesh axis runs over, the one named last changes fastest.
Arguments:
- curvature: float32 [32, 1024, 4096], P(None, 'row', 'col'), may hold values from -4 to 7, as said below
Outputs:
- factored: float32 [32, 1024, 4096], P(None, 'row', 'col')
The draws below stay inside these ranges and needn't reach their ends.
Inputs may be any that keep to these rules, and one draw needn't show every extreme that they name: `curvature`: rows 0 to 4095, read as a square matrix, are symmetric positive definite with smallest eigenvalue at least 0.5.
All inputs are finite; a program needn't handle non-finite values.
Results may differ from the reference program's by a relative error of at most 0.0014.
Values may be sent and summed in bfloat16 or wider, within the bound.
A program may use at most 192 MiB of HBM per device.

```python
import math
import jax
import jax.numpy as jnp
from jax import lax

MATRIX = 32768
PANEL = 1024
STEPS = 2
CYCLES = 32
N_COL = 4


def draw_curvature(key, part):
    slab_width = N_COL * PANEL
    gram_rows = slab_width // 2
    key_jacobian = jax.random.fold_in(key, 101)
    key_bottom = jax.random.fold_in(key, 202)
    key_damping = jax.random.fold_in(key, 303)
    jacobian = jnp.clip(jax.random.normal(key_jacobian, (gram_rows, slab_width), jnp.float32), -4.0, 4.0)
    bottom = jnp.clip(jax.random.normal(key_bottom, (MATRIX - slab_width, slab_width), jnp.float32), -4.0, 4.0)
    gram = jnp.dot(jacobian.T, jacobian, precision=lax.Precision.HIGHEST, preferred_element_type=jnp.float32) / gram_rows
    gram = 0.5 * (gram + gram.T)
    damping = jnp.exp(jax.random.uniform(key_damping, (slab_width,), jnp.float32, math.log(0.5), math.log(2.0)))
    identity = jnp.eye(slab_width, dtype=jnp.float32)
    top_block = gram + identity * damping[None, :]
    whole = jnp.concatenate([top_block, bottom], 0)
    return whole.reshape(MATRIX // PANEL, PANEL, slab_width)


def setup_inputs(seed: int = 0) -> dict:
    splits = jax.random.split(jax.random.key(seed), 2)
    curvature = draw_curvature(jax.random.fold_in(splits[1], 71), 0)
    return dict(curvature=curvature)


def reference(curvature):
    slab_width = N_COL * PANEL
    matrix = curvature.reshape(MATRIX, slab_width)
    for step in range(STEPS):
        lower_edge = step * PANEL
        upper_edge = lower_edge + PANEL
        factor = jnp.linalg.cholesky(matrix[lower_edge:upper_edge, lower_edge:upper_edge])
        solved = jax.scipy.linalg.solve_triangular(factor, matrix[upper_edge:, lower_edge:upper_edge].T, lower=True).T
        panel_new = jnp.concatenate([jnp.zeros((lower_edge, PANEL), matrix.dtype), factor, solved], 0)
        matrix = matrix.at[:, lower_edge:upper_edge].set(panel_new)
        rounded = lax.optimization_barrier(solved.astype(jnp.bfloat16)).astype(jnp.float32)
        update = jnp.dot(rounded.astype(jnp.float32), rounded[:slab_width - upper_edge].T.astype(jnp.float32), precision=lax.Precision.HIGHEST, preferred_element_type=jnp.float32)
        matrix = matrix.at[upper_edge:, upper_edge:].add(-update)
    row_ids = lax.broadcasted_iota(jnp.int32, (MATRIX, slab_width), 0)
    col_ids = lax.broadcasted_iota(jnp.int32, (MATRIX, slab_width), 1)
    blanked = (row_ids < STEPS * PANEL) & (col_ids >= STEPS * PANEL)
    matrix = jnp.where(blanked, jnp.zeros_like(matrix), matrix)
    return matrix.reshape(CYCLES, PANEL, slab_width)
```

```python
import jax
import jax.numpy as jnp
from jax import lax
from jax.sharding import PartitionSpec as P

BLOCK = 128
HIGH = lax.Precision.HIGH
HIGHEST = lax.Precision.HIGHEST


def from_root(x, axis, root):
    mine = lax.axis_index(axis) == root
    return lax.psum(jnp.where(mine, x, jnp.zeros_like(x)), axis)


def nt(left, right, precision=None):
    return lax.dot_general(
        left,
        right,
        (((1,), (1,)), ((), ())),
        precision=precision,
        preferred_element_type=jnp.float32,
    )


def nn(left, right):
    return lax.dot_general(
        left,
        right,
        (((1,), (0,)), ((), ())),
        precision=HIGHEST,
        preferred_element_type=jnp.float32,
    )


def factor_and_inverse(block):
    n = block.shape[0]
    width = min(BLOCK, n)
    rest = 0.5 * (block + block.T)
    identity = jnp.eye(width, dtype=jnp.float32)
    columns, inverses = [], []
    for start in range(0, n, width):
        small = lax.linalg.cholesky(rest[:width, :width], symmetrize_input=False)
        inverse = jax.scipy.linalg.solve_triangular(small, identity, lower=True)
        inverses.append(inverse)
        pieces = [jnp.zeros((start, width), jnp.float32)] if start else []
        pieces.append(small)
        if start + width < n:
            below = nt(rest[width:, :width], inverse, HIGHEST)
            rest = rest[width:, width:] - nt(below, below, HIGHEST)
            pieces.append(below)
        columns.append(jnp.concatenate(pieces, 0))
    factor = jnp.concatenate(columns, 1)
    size = width
    while len(inverses) > 1:
        merged = []
        for i in range(0, len(inverses), 2):
            top, bottom = inverses[i], inverses[i + 1]
            at = i * size
            corner = factor[at + size : at + 2 * size, at : at + size]
            left = -nn(bottom, nn(corner, top))
            merged.append(
                jnp.concatenate(
                    [
                        jnp.concatenate([top, jnp.zeros_like(top)], 1),
                        jnp.concatenate([left, bottom], 1),
                    ],
                    0,
                )
            )
        inverses = merged
        size *= 2
    return factor, inverses[0]


def on_device(curvature):
    cycles, tile, width = curvature.shape
    row = lax.axis_index("row")
    col = lax.axis_index("col")

    def gather_rows(piece):
        return lax.all_gather(piece, "row", axis=0, tiled=True)

    def own_rows(matrix):
        return lax.dynamic_slice_in_dim(matrix, row * tile, tile, 0)

    block00 = gather_rows(from_root(curvature[0], "col", 0))
    head = from_root(jnp.stack([curvature[0], curvature[1]], 0), "col", 1)
    block01 = gather_rows(head[0])
    block11 = gather_rows(head[1])
    mine0 = gather_rows(curvature[0])
    mine1 = gather_rows(curvature[1])

    factor0, inverse0 = factor_and_inverse(block00)
    below = curvature[1:].reshape((cycles - 1) * tile, width)
    solved0 = nt(below, inverse0, HIGH)
    sent0 = solved0.astype(jnp.bfloat16)
    sent0, block11, block01 = lax.optimization_barrier((sent0, block11, block01))
    panel0 = from_root(sent0, "col", 0)

    next0 = nn(inverse0, block01).astype(jnp.bfloat16)
    facing0 = nn(inverse0, mine0).astype(jnp.bfloat16)

    def tn(left, right):
        return lax.dot_general(
            left, right, (((0,), (0,)), ((), ())), preferred_element_type=jnp.float32
        )

    factor1, inverse1 = factor_and_inverse(block11 - tn(next0, next0))
    facing1 = nn(inverse1, mine1 - tn(next0, facing0)).astype(jnp.bfloat16)

    def plain(left, right):
        return lax.dot_general(
            left, right, (((1,), (0,)), ((), ())), preferred_element_type=jnp.float32
        )

    state = jnp.where(col == 0, solved0, below - plain(panel0, facing0))
    low = state[tile:]
    solved1 = nt(low, inverse1, HIGH)
    panel1 = from_root(solved1.astype(jnp.bfloat16), "col", 1)
    low = jnp.where(
        col == 1, solved1, jnp.where(col > 1, low - plain(panel1, facing1), low)
    )
    zeros = jnp.zeros((tile, width), jnp.float32)
    first = jnp.where(col == 0, own_rows(factor0), zeros)
    second = jnp.where(
        col == 0, state[:tile], jnp.where(col == 1, own_rows(factor1), zeros)
    )
    return jnp.concatenate([first, second, low], 0).reshape(cycles, tile, width)


def solution(mesh):
    in_specs = (P(None, "row", "col"),)
    out_specs = P(None, "row", "col")
    return jax.shard_map(
        on_device, mesh=mesh, in_specs=in_specs, out_specs=out_specs, check_vma=False
    )
```
